256 devices in a mesh: row: 4 (over z_lo, core), col: 64 (over y, x, z_hi).
Axes of the slice: x: 4, y: 4, z: 8 (z_hi: 4, z_lo: 2; z = z_hi * 2 + z_lo), core: 2. Of those that a mesh axis runs over, the one named last changes fastest.
Arguments:
- matrix_t: bfloat16 [30720, 30720], P('col', 'row')
- fibers: float32 [3, 131072], P(None, 'col'), may hold values from -0.7 to 0.7, as said below
- forces: float32 [3, 131072], P(None, 'col'), may hold values from -0.375 to 0.375
- nodes: float32 [3, 10240], P(None, 'row'), may hold values from -1 to 1, as said below
- node_order: int32 [10240], replicated, may hold values from 0 to 10239, each once
Outputs:
- velocity: float32 [30720], P(('row', 'col'))
- density: float32 [30720], P(('row', 'col'))
The draws below stay inside these ranges and needn't reach their ends.
Inputs may be any that keep to these rules, and one draw needn't show every extreme that they name: node_order holds every number below 10240 once. `nodes`: every node lies on the unit sphere about the anchor. `fibers`: every fiber point lies within distance 0.7 of the anchor.
All inputs are finite; a program needn't handle non-finite values.
Results may differ from the reference program's by a relative error of at most 0.00067.
Values may be sent and summed in bfloat16 or wider, within the bound.
A program may use at most 64 MiB of HBM per device.

```python
import math
import jax
import jax.numpy as jnp
from jax import lax

NP = 10240
ORDER = 30720
NF = 131072


def sign_fields(key, count, length):
    flips = jax.random.bernoulli(key, 0.5, (count, length))
    return jnp.where(flips, 1.0, -1.0).astype(jnp.float32)


def draw_matrix_t(key, part):
    noise_key = jax.random.fold_in(key, 21)
    scale_key = jax.random.fold_in(key, 22)
    field_key = jax.random.fold_in(key, 23)
    strength = 0.35
    first_gain = 0.5
    second_gain = 1.0
    values = jax.random.normal(noise_key, (ORDER, ORDER), jnp.float32)
    mean_square = 15.0 / math.log(16.0)
    row_scale = jnp.exp(jax.random.uniform(scale_key, (ORDER,), jnp.float32, 0.0, 1.0) * math.log(4.0))
    spread = strength / (math.sqrt(ORDER) * mean_square)
    signs = sign_fields(field_key, 6, ORDER)
    component = jnp.arange(ORDER) % 3
    feed = jnp.where(component[:, None] == 0, signs[0][None, :], jnp.where(component[:, None] == 1, signs[1][None, :], signs[2][None, :]))
    chained = signs[0][:, None] * signs[3][None, :] + signs[1][:, None] * signs[4][None, :]
    chained = chained + signs[2][:, None] * signs[5][None, :]
    scaled = values * row_scale[:, None] * row_scale[None, :] * spread
    matrix = scaled + feed * (first_gain * math.sqrt(3.0) / ORDER) + chained * (second_gain / ORDER)
    return matrix.astype(jnp.bfloat16)


def sphere_points(key, count):
    height = jax.random.uniform(jax.random.fold_in(key, 1), (count,), jnp.float32, -1.0, 1.0)
    angle_val = jax.random.uniform(jax.random.fold_in(key, 2), (count,), jnp.float32, -math.pi, math.pi)
    planar = jnp.sqrt(jnp.maximum(1.0 - height * height, 0.0))
    return jnp.stack([planar * jnp.cos(angle_val), planar * jnp.sin(angle_val), height])


def draw_nodes(key, part):
    return sphere_points(key, NP)


def draw_fibers(key, part):
    direction = sphere_points(jax.random.fold_in(key, 7), NF)
    radius_val = 0.7 * jax.random.uniform(jax.random.fold_in(key, 9), (NF,), jnp.float32, 0.0, 1.0) ** (1.0 / 3.0)
    return direction * radius_val[None, :]


def level_of(stream_key, shape, shards, low, top_value):
    def one(position, parts):
        steps = jax.random.uniform(jax.random.fold_in(jax.random.fold_in(stream_key, 6), position), (parts,), jnp.float32, low / len(shards), top_value / len(shards))
        return jnp.repeat(jnp.exp(steps), shape[position] // parts).reshape((-1,) + (1,) * (len(shape) - position - 1))

    loudness = one(*shards[0])
    for cut in shards[1:]:
        loudness = loudness * one(*cut)
    return loudness


def scatter_about(own_key, dims, deviation, most, split=(), held_as=jnp.bfloat16):
    gain = level_of(own_key, dims, split, -0.22, 0.18) if split else 1.0
    drawn = jax.random.normal(own_key, dims, jnp.float32) * deviation * gain
    return jnp.minimum(jnp.maximum(drawn, -most), most).astype(held_as)


def setup_inputs(seed: int = 0) -> dict:
    key_list = jax.random.split(jax.random.key(seed), 6)
    return {
        "matrix_t": draw_matrix_t(jax.random.fold_in(key_list[5], 71), 0),
        "fibers": draw_fibers(jax.random.fold_in(key_list[5], 71), 0),
        "forces": scatter_about(key_list[2], (3, NF), 0.06, 0.375, ((1, 64),), jnp.float32),
        "nodes": draw_nodes(jax.random.fold_in(key_list[5], 71), 0),
        "node_order": jax.random.permutation(key_list[4], NP).astype(jnp.int32),
    }


inv_eight_pi = 1.0 / (8.0 * math.pi)
tiny_eps = 1e-06

def stokeslet_sum(targets, sources, strengths):
    count_src = sources.shape[1]
    width_blk = math.gcd(count_src, 1024)
    source_blocks = sources.reshape(3, count_src // width_blk, width_blk).transpose(1, 0, 2)
    force_blocks = strengths.reshape(3, count_src // width_blk, width_blk).transpose(1, 0, 2)

    def advance(running, paired):
        source, force_block = paired
        offset = targets[:, None, :] - source[:, :, None]
        inverse = 1.0 / jnp.sqrt(lax.optimization_barrier(jnp.sum(offset * offset, axis=0)))
        projected = lax.optimization_barrier(jnp.sum(offset * force_block[:, :, None], axis=0)) * (inverse * inverse * inverse)
        return (running + lax.optimization_barrier(jnp.sum(force_block[:, :, None] * inverse[None] + offset * projected[None], axis=1)), None)
    running, unused = lax.scan(advance, jnp.zeros(targets.shape, jnp.float32), (source_blocks, force_blocks))
    return running * inv_eight_pi

def apply_operator(vector, matrix_t):
    order_total = vector.shape[0]
    width_blk = math.gcd(order_total, 1024)
    row_blocks = matrix_t.reshape(order_total // width_blk, width_blk, order_total)
    vector_blocks = vector.astype(jnp.bfloat16).reshape(order_total // width_blk, width_blk)

    def advance(running, paired):
        return (running + jnp.dot(paired[0], paired[1], preferred_element_type=jnp.float32), None)
    running, unused = lax.scan(advance, jnp.zeros((order_total,), jnp.float32), (vector_blocks, row_blocks))
    return vector + running

def givens_solve(initial_norm, entry_11, entry_21, entry_12, entry_22, entry_32):
    radius_one = jnp.sqrt(entry_11 * entry_11 + entry_21 * entry_21)
    cosine_one = entry_11 / radius_one
    sine_one = entry_21 / radius_one
    upper_12 = cosine_one * entry_12 + sine_one * entry_22
    lower_22 = cosine_one * entry_22 - sine_one * entry_12
    radius_two = jnp.sqrt(lower_22 * lower_22 + entry_32 * entry_32)
    weight_two = lower_22 / radius_two * (-sine_one * initial_norm) / radius_two
    weight_one = (cosine_one * initial_norm - upper_12 * weight_two) / radius_one
    return (weight_one, weight_two)

def reference(matrix_t, fibers, forces, nodes, node_order):
    targets = jnp.take(nodes, node_order, axis=1)
    velocity = stokeslet_sum(targets, fibers, forces).T.reshape(-1)
    initial_norm = jnp.sqrt(jnp.sum(velocity * velocity) + tiny_eps)
    basis_one = velocity / initial_norm
    image_one = apply_operator(basis_one, matrix_t)
    entry_11 = jnp.sum(basis_one * image_one)
    rest_one = image_one - entry_11 * basis_one
    entry_21 = jnp.sqrt(jnp.sum(rest_one * rest_one) + tiny_eps)
    basis_two = rest_one / entry_21
    image_two = apply_operator(basis_two, matrix_t)
    entry_12 = jnp.sum(basis_one * image_two)
    partial_two = image_two - entry_12 * basis_one
    entry_22 = jnp.sum(basis_two * partial_two)
    rest_two = partial_two - entry_22 * basis_two
    entry_32 = jnp.sqrt(jnp.sum(rest_two * rest_two) + tiny_eps)
    weight_one, weight_two = givens_solve(initial_norm, entry_11, entry_21, entry_12, entry_22, entry_32)
    density = weight_one * basis_one + weight_two * basis_two
    return (velocity, density)
```

```python
import functools
import math

import jax
import jax.numpy as jnp
from jax import lax
from jax.experimental import pallas as pl
from jax.experimental.pallas import tpu as pltpu
from jax.sharding import PartitionSpec as P

MESH = pl.DeviceIdType.MESH
inv_eight_pi = 1.0 / (8.0 * math.pi)
tiny_eps = 1e-06
f32 = jnp.float32
bf16 = jnp.bfloat16

ROWS = 4
COLS = 64
TARGETS = 2560
SOURCES = 2048
BLOCK = 480
WIDTH = 7680
PLANE = 16


def pieces_of(value, count):
    found = []
    rest = value
    for _ in range(count):
        piece = rest.astype(bf16).astype(f32)
        found.append(piece)
        rest = rest - piece
    return found


def spread_nodes(nodes_ref, all_ref, send_sem, recv_sem, own_sem):
    row = lax.axis_index("row")
    barrier = pltpu.get_barrier_semaphore()
    for step in range(1, ROWS):
        other = lax.rem(row + step, ROWS)
        pl.semaphore_signal(
            barrier, inc=1, device_id={"row": other}, device_id_type=MESH
        )
    own = pltpu.make_async_copy(nodes_ref, all_ref.at[row], own_sem)
    own.start()
    pl.semaphore_wait(barrier, ROWS - 1)
    copies = []
    for step in range(1, ROWS):
        other = lax.rem(row + step, ROWS)
        copy = pltpu.make_async_remote_copy(
            src_ref=nodes_ref,
            dst_ref=all_ref.at[row],
            send_sem=send_sem.at[step],
            recv_sem=recv_sem.at[step],
            device_id={"row": other},
            device_id_type=MESH,
        )
        copy.start()
        copies.append(copy)
    own.wait()
    for copy in copies:
        copy.wait()


def stokes_kernel(
    nodes_ref,
    order_ref,
    fibers_ref,
    forces_ref,
    out_ref,
    index_ref,
    target_ref,
    feature_ref,
    column_ref,
    source_ref,
    pull_ref,
    weight_f,
    weight_s,
    sum_f,
    sum_s,
):
    row = lax.axis_index("row")
    index_ref[pl.ds(0, 20), :] = order_ref[row]
    index_ref[pl.ds(20, 4), :] = jnp.zeros((4, 128), jnp.int32)
    index = index_ref[...]
    high = index // 128
    low = index - high * 128
    found = tuple(jnp.zeros((24, 128), f32) for _ in range(3))

    def pick(part, found):
        found = list(found)
        for tile in range(20):
            hit = high == part * 20 + tile
            for k in range(3):
                line = nodes_ref[part, pl.ds(k, 1), pl.ds(tile * 128, 128)]
                line = jnp.broadcast_to(line, (24, 128))
                taken = jnp.take_along_axis(line, low, axis=1)
                found[k] = jnp.where(hit, taken, found[k])
        return tuple(found)

    found = lax.fori_loop(0, ROWS, pick, found)
    square = found[0] * found[0] + found[1] * found[1] + found[2] * found[2]
    lines = []
    for k in range(3):
        one, two, three = pieces_of(found[k], 3)
        lines += [one, two, one, three, one, two]
    lines += pieces_of(square, 3)
    feature_ref[...] = jnp.ones((32, TARGETS), f32)
    for slot, line in enumerate(lines):
        for tile in range(20):
            feature_ref[pl.ds(slot, 1), pl.ds(tile * 128, 128)] = line[tile : tile + 1]
    for k in range(3):
        for tile in range(20):
            target_ref[pl.ds(k, 1), pl.ds(tile * 128, 128)] = found[k][tile : tile + 1]
    column_ref[...] = feature_ref[...].astype(bf16)

    fibers = fibers_ref[...]
    forces = forces_ref[...]
    place = [fibers[k : k + 1] for k in range(3)]
    force = [forces[k : k + 1] for k in range(3)]
    source_square = place[0] * place[0] + place[1] * place[1] + place[2] * place[2]
    source_dot = place[0] * force[0] + place[1] * force[1] + place[2] * force[2]
    nought = jnp.zeros((1, SOURCES), f32)
    unit = jnp.ones((1, SOURCES), f32)

    def stack(parts, tail, total):
        rows = []
        for k in range(3):
            one, two, three = pieces_of(parts[k], 3)
            rows += [one, one, two, one, three, two]
        rows += tail + pieces_of(total, 3) + [nought] * 8
        return jnp.concatenate(rows, axis=0)

    near = stack([-2.0 * one for one in place], [unit] * 3, source_square)
    turn = stack(force, [nought] * 3, -source_dot)
    source_ref[...] = near.T.astype(bf16)
    pull_ref[...] = turn.T.astype(bf16)
    force_pieces = [pieces_of(one, 2) for one in force]
    place_pieces = [pieces_of(one, 2) for one in place]
    weight_f[...] = jnp.concatenate(
        [one[0] for one in force_pieces]
        + [one[1] for one in force_pieces]
        + [nought] * 10,
        axis=0,
    ).astype(bf16)
    weight_s[...] = jnp.concatenate(
        [one[0] for one in place_pieces]
        + [one[1] for one in place_pieces]
        + [unit]
        + [nought] * 9,
        axis=0,
    ).astype(bf16)
    sum_f[...] = jnp.zeros((16, TARGETS), f32)
    sum_s[...] = jnp.zeros((16, TARGETS), f32)
    wide = 512
    deep = 256

    def advance(turn_index, carry):
        at = pl.ds(pl.multiple_of((turn_index // (SOURCES // deep)) * wide, wide), wide)
        of = pl.ds(
            pl.multiple_of(lax.rem(turn_index, SOURCES // deep) * deep, deep), deep
        )
        columns = column_ref[:, at]
        square = jnp.dot(source_ref[of, :], columns, preferred_element_type=f32)
        along = jnp.dot(pull_ref[of, :], columns, preferred_element_type=f32)
        inverse = lax.rsqrt(square)
        projected = along * (inverse * inverse * inverse)
        inverse_high = inverse.astype(bf16)
        inverse_low = (inverse - inverse_high.astype(f32)).astype(bf16)
        projected_high = projected.astype(bf16)
        projected_low = (projected - projected_high.astype(f32)).astype(bf16)
        with_f = weight_f[:, of]
        with_s = weight_s[:, of]
        sum_f[:, at] += jnp.dot(
            with_f, inverse_high, preferred_element_type=f32
        ) + jnp.dot(with_f, inverse_low, preferred_element_type=f32)
        sum_s[:, at] += jnp.dot(
            with_s, projected_high, preferred_element_type=f32
        ) + jnp.dot(with_s, projected_low, preferred_element_type=f32)
        return carry

    lax.fori_loop(0, (TARGETS // wide) * (SOURCES // deep), advance, 0)
    total_f = sum_f[...]
    total_s = sum_s[...]
    for k in range(3):
        value = (
            total_f[k : k + 1]
            + total_f[3 + k : 4 + k]
            + target_ref[pl.ds(k, 1), :] * total_s[6:7]
            - (total_s[k : k + 1] + total_s[3 + k : 4 + k])
        ) * inv_eight_pi
        for tile in range(20):
            out_ref[tile * 3 + k] = value[:, tile * 128 : tile * 128 + 128]


def total_of(value):
    return jnp.sum(value, axis=1, keepdims=True)


def krylov_kernel(
    part_ref,
    matrix_ref,
    velocity_ref,
    density_ref,
    held,
    image_one,
    image_two,
    recv_one,
    recv_two,
    recv_three,
    dots,
    recv_dots,
    piece,
    recv_piece,
    spread,
    load_sem,
    send_sems,
    recv_sems,
    dot_send,
    dot_recv,
    piece_send,
    piece_recv,
):
    row = lax.axis_index("row")
    col = lax.axis_index("col")
    level = col // PLANE
    inside = lax.rem(col, PLANE)
    load = pltpu.make_async_copy(matrix_ref, held, load_sem)
    load.start()
    piece_row = level
    piece_col = inside * 4 + row
    piece_own = jnp.logical_and(piece_row == row, piece_col == col)
    from_row = lax.rem(col, 4)
    from_col = row * PLANE + col // 4
    self_in = level == row

    barrier = pltpu.get_barrier_semaphore()

    def greet(step, carry):
        other = lax.rem(col + step, COLS)

        @pl.when(jnp.logical_not(jnp.logical_and(level == row, step == 0)))
        def _():
            pl.semaphore_signal(
                barrier, inc=1, device_id=(level, other), device_id_type=MESH
            )

        @pl.when(step > 0)
        def _():
            pl.semaphore_signal(
                barrier, inc=1, device_id=(row, other), device_id_type=MESH
            )

        return carry

    lax.fori_loop(0, COLS, greet, 0)

    @pl.when(jnp.logical_not(piece_own))
    def _():
        pl.semaphore_signal(
            barrier, inc=1, device_id=(from_row, from_col), device_id_type=MESH
        )

    lane_node = lax.broadcasted_iota(jnp.int32, (256, 512), 0)
    lane_entry = lax.broadcasted_iota(jnp.int32, (256, 512), 1)
    base = lane_entry - 3 * (lane_node - 32 * lax.rem(col, 4))
    for k in range(3):
        spread[k] = jnp.where(
            jnp.logical_and(base == k, lane_entry < BLOCK), 1.0, 0.0
        ).astype(bf16)

    peers = 2 * COLS - self_in.astype(jnp.int32) - piece_own.astype(jnp.int32)
    pl.semaphore_wait(barrier, peers)

    def send_blocks(stage, source, target, stride, scale, count):
        def one(step, carry):
            place = lax.rem(step + col, COLS)
            block = place // 4
            to_row = lax.rem(place, 4)
            to_col = row * PLANE + block
            window = source.at[pl.ds((stride * block) // 4 * scale, count)]
            is_self = jnp.logical_and(to_row == row, to_col == col)

            @pl.when(is_self)
            def _():
                pltpu.make_async_copy(
                    window, target.at[col], recv_sems.at[stage]
                ).start()

            @pl.when(jnp.logical_not(is_self))
            def _():
                pltpu.make_async_remote_copy(
                    src_ref=window,
                    dst_ref=target.at[col],
                    send_sem=send_sems.at[stage],
                    recv_sem=recv_sems.at[stage],
                    device_id=(to_row, to_col),
                    device_id_type=MESH,
                ).start()

            return carry

        lax.fori_loop(0, COLS, one, 0)

    def await_blocks(stage, target):
        pltpu.make_async_copy(target, target, recv_sems.at[stage]).wait()

    def await_sent(stage, target):
        @pl.when(self_in)
        def _():
            some = target.at[pl.ds(0, COLS - 1)]
            pltpu.make_async_copy(some, some, send_sems.at[stage]).wait()

        @pl.when(jnp.logical_not(self_in))
        def _():
            pltpu.make_async_copy(target, target, send_sems.at[stage]).wait()

    def added(target):
        def one(step, running):
            return running + target[step]

        return lax.fori_loop(1, COLS, one, target[0], unroll=9)

    def send_piece(which, vector):
        chosen = vector[:, 0:128]
        for quarter in range(1, 4):
            chosen = jnp.where(
                row == quarter, vector[:, 120 * quarter : 120 * quarter + 128], chosen
            )
        piece[which] = chosen

        @pl.when(piece_own)
        def _():
            pltpu.make_async_copy(
                piece.at[which], recv_piece.at[which], piece_recv.at[which]
            ).start()

        @pl.when(jnp.logical_not(piece_own))
        def _():
            pltpu.make_async_remote_copy(
                src_ref=piece.at[which],
                dst_ref=recv_piece.at[which],
                send_sem=piece_send.at[which],
                recv_sem=piece_recv.at[which],
                device_id=(piece_row, piece_col),
                device_id_type=MESH,
            ).start()

    def await_piece(which):
        pltpu.make_async_copy(
            recv_piece.at[which], recv_piece.at[which], piece_recv.at[which]
        ).wait()

        @pl.when(jnp.logical_not(piece_own))
        def _():
            pltpu.make_async_copy(
                recv_piece.at[which], recv_piece.at[which], piece_send.at[which]
            ).wait()

    lane = lax.broadcasted_iota(jnp.int32, (1, 128), 1)

    def send_dots(which, values):
        line = jnp.zeros((1, 128), f32)
        for slot, value in enumerate(values):
            line = jnp.where(lane == slot, value, line)
        dots[which] = line

        def one(step, carry):
            pltpu.make_async_remote_copy(
                src_ref=dots.at[which],
                dst_ref=recv_dots.at[which, step - 1],
                send_sem=dot_send.at[which],
                recv_sem=dot_recv.at[which],
                device_id=(row, lax.rem(col + step, COLS)),
                device_id_type=MESH,
            ).start()
            return carry

        lax.fori_loop(1, COLS, one, 0)

    def await_dots(which, count):
        whole = recv_dots.at[which]
        pltpu.make_async_copy(whole, whole, dot_recv.at[which]).wait()

        def one(step, running):
            return running + recv_dots[which, step]

        line = lax.fori_loop(0, COLS - 1, one, dots[which], unroll=9)
        return [total_of(jnp.where(lane == slot, line, 0.0)) for slot in range(count)]

    def await_dots_sent(which):
        whole = recv_dots.at[which]
        pltpu.make_async_copy(whole, whole, dot_send.at[which]).wait()

    which_row = lax.broadcasted_iota(jnp.int32, (16, 512), 0)

    def multiply(vector, image):
        high, low = pieces_of(vector, 2)
        left = jnp.where(which_row == 0, high, jnp.where(which_row == 1, low, 0.0))
        left = left.astype(bf16)[:, :BLOCK]

        for step in range(WIDTH // 512):
            got = jnp.dot(
                left, held[:, step * 512 : step * 512 + 512], preferred_element_type=f32
            )
            got = got[0:1] + got[1:2]
            for tile in range(4):
                image[step * 4 + tile] = got[:, tile * 128 : tile * 128 + 128]

    offset = lax.rem(96 * lax.rem(col, 4), 128)
    lane_wide = lax.broadcasted_iota(jnp.int32, (1, 512), 1)

    def aligned(total):
        line = jnp.concatenate([total[tile] for tile in range(5)], axis=1)
        chosen = line[:, 0:512]
        for shift in (32, 64, 96):
            chosen = jnp.where(offset == shift, line[:, shift : shift + 512], chosen)
        return jnp.where(lane_wide < BLOCK, chosen, 0.0)

    send_blocks(0, part_ref, recv_one, 5, 3, 6)
    image_one[WIDTH // 128] = jnp.zeros((1, 128), f32)
    image_two[WIDTH // 128] = jnp.zeros((1, 128), f32)
    await_blocks(0, recv_one)
    total = added(recv_one)
    which_small = lax.broadcasted_iota(jnp.int32, (16, 256), 0)
    first = jnp.zeros((16, 512), f32)
    for k in range(3):
        line = jnp.concatenate([total[k], total[3 + k]], axis=1)
        one, two, three = pieces_of(line, 3)
        left = jnp.where(
            which_small == 0,
            one,
            jnp.where(which_small == 1, two, jnp.where(which_small == 2, three, 0.0)),
        )
        first = first + jnp.dot(
            left.astype(bf16), spread[k], preferred_element_type=f32
        )
    vector = first[0:1] + first[1:2] + first[2:3]
    load.wait()
    multiply(vector, image_one)
    send_blocks(1, image_one, recv_two, 15, 1, 5)
    send_piece(0, vector)
    await_blocks(1, recv_two)
    image = aligned(added(recv_two))
    multiply(image, image_two)
    send_blocks(2, image_two, recv_three, 15, 1, 5)
    send_piece(1, image)
    send_dots(
        0, [total_of(vector * vector), total_of(vector * image), total_of(image * image)]
    )
    vv, vw, ww = await_dots(0, 3)
    norm_square = vv + tiny_eps
    initial_norm = jnp.sqrt(norm_square)
    scale_one = 1.0 / initial_norm
    entry_11 = (vv + vw) / norm_square
    slide = (vw - tiny_eps) / norm_square
    rest_square = (ww - 2.0 * slide * vw + slide * slide * vv) / norm_square
    entry_21 = jnp.sqrt(jnp.maximum(rest_square, 0.0) + tiny_eps)
    scale_two = scale_one / entry_21
    basis_one = vector * scale_one
    basis_two = (image - slide * vector) * scale_two
    await_blocks(2, recv_three)
    last = (aligned(added(recv_three)) - slide * image) * scale_two
    send_dots(
        1,
        [
            total_of(basis_one * basis_one),
            total_of(basis_one * basis_two),
            total_of(basis_two * basis_two),
            total_of(basis_one * last),
            total_of(basis_two * last),
            total_of(last * last),
        ],
    )
    await_piece(0)
    await_piece(1)
    velocity_piece = recv_piece[0]
    image_piece = recv_piece[1]
    velocity_ref[...] = velocity_piece[:, :120]
    aa, ab, bb, al, bl, ll = await_dots(1, 6)
    entry_12 = ab + al
    entry_22 = bb + bl - entry_12 * ab
    from_one = -entry_12
    from_two = 1.0 - entry_22
    rest_two = (
        ll
        + from_one * from_one * aa
        + from_two * from_two * bb
        + 2.0 * (from_one * from_two * ab + from_one * al + from_two * bl)
    )
    entry_32 = jnp.sqrt(jnp.maximum(rest_two, 0.0) + tiny_eps)
    radius_one = jnp.sqrt(entry_11 * entry_11 + entry_21 * entry_21)
    cosine_one = entry_11 / radius_one
    sine_one = entry_21 / radius_one
    upper_12 = cosine_one * entry_12 + sine_one * entry_22
    lower_22 = cosine_one * entry_22 - sine_one * entry_12
    radius_two = jnp.sqrt(lower_22 * lower_22 + entry_32 * entry_32)
    weight_two = lower_22 / radius_two * (-sine_one * initial_norm) / radius_two
    weight_one = (cosine_one * initial_norm - upper_12 * weight_two) / radius_one
    result = weight_one * (velocity_piece * scale_one) + weight_two * (
        (image_piece - slide * velocity_piece) * scale_two
    )
    density_ref[...] = result[:, :120]
    await_sent(0, recv_one)
    await_sent(1, recv_two)
    await_sent(2, recv_three)
    await_dots_sent(0)
    await_dots_sent(1)


def in_vmem(count):
    return [pl.BlockSpec(memory_space=pltpu.VMEM)] * count


def shards(matrix_t, fibers, forces, nodes, node_order):
    all_nodes = pl.pallas_call(
        spread_nodes,
        name="spread_nodes",
        out_shape=jax.ShapeDtypeStruct((ROWS, 3, TARGETS), f32),
        in_specs=in_vmem(1),
        out_specs=in_vmem(1)[0],
        scratch_shapes=[
            pltpu.SemaphoreType.DMA((ROWS,)),
            pltpu.SemaphoreType.DMA((ROWS,)),
            pltpu.SemaphoreType.DMA,
        ],
        compiler_params=pltpu.CompilerParams(collective_id=0, has_side_effects=True),
    )(nodes)
    part = pl.pallas_call(
        stokes_kernel,
        name="stokes",
        out_shape=jax.ShapeDtypeStruct((TARGETS * 3 // 128, 1, 128), f32),
        in_specs=in_vmem(4),
        out_specs=in_vmem(1)[0],
        scratch_shapes=[
            pltpu.VMEM((24, 128), jnp.int32),
            pltpu.VMEM((8, TARGETS), f32),
            pltpu.VMEM((32, TARGETS), f32),
            pltpu.VMEM((32, TARGETS), bf16),
            pltpu.VMEM((SOURCES, 32), bf16),
            pltpu.VMEM((SOURCES, 32), bf16),
            pltpu.VMEM((16, SOURCES), bf16),
            pltpu.VMEM((16, SOURCES), bf16),
            pltpu.VMEM((16, TARGETS), f32),
            pltpu.VMEM((16, TARGETS), f32),
        ],
    )(all_nodes, node_order.reshape(ROWS, 20, 128), fibers, forces)
    velocity, density = pl.pallas_call(
        krylov_kernel,
        name="krylov",
        out_shape=[jax.ShapeDtypeStruct((1, 120), f32)] * 2,
        in_specs=in_vmem(1) + [pl.BlockSpec(memory_space=pl.ANY)],
        out_specs=in_vmem(2),
        scratch_shapes=[
            pltpu.VMEM((BLOCK, WIDTH), bf16),
            pltpu.VMEM((WIDTH // 128 + 1, 1, 128), f32),
            pltpu.VMEM((WIDTH // 128 + 1, 1, 128), f32),
            pltpu.VMEM((COLS, 6, 1, 128), f32),
            pltpu.VMEM((COLS, 5, 1, 128), f32),
            pltpu.VMEM((COLS, 5, 1, 128), f32),
            pltpu.VMEM((2, 1, 128), f32),
            pltpu.VMEM((2, COLS - 1, 1, 128), f32),
            pltpu.VMEM((2, 1, 128), f32),
            pltpu.VMEM((2, 1, 128), f32),
            pltpu.VMEM((3, 256, 512), bf16),
            pltpu.SemaphoreType.DMA,
            pltpu.SemaphoreType.DMA((3,)),
            pltpu.SemaphoreType.DMA((3,)),
            pltpu.SemaphoreType.DMA((2,)),
            pltpu.SemaphoreType.DMA((2,)),
            pltpu.SemaphoreType.DMA((2,)),
            pltpu.SemaphoreType.DMA((2,)),
        ],
        compiler_params=pltpu.CompilerParams(collective_id=1, has_side_effects=True),
    )(part, matrix_t)
    return velocity.reshape(120), density.reshape(120)


def solution(mesh):
    return jax.shard_map(
        shards,
        mesh=mesh,
        in_specs=(P("col", "row"), P(None, "col"), P(None, "col"), P(None, "row"), P()),
        out_specs=(P(("row", "col")), P(("row", "col"))),
        check_vma=False,
    )
```

```python
import functools
import math

import jax
import jax.numpy as jnp
from jax import lax
from jax.experimental import pallas as pl
from jax.experimental.pallas import tpu as pltpu
from jax.sharding import PartitionSpec as P

MESH = pl.DeviceIdType.MESH
inv_eight_pi = 1.0 / (8.0 * math.pi)
tiny_eps = 1e-06
f32 = jnp.float32
bf16 = jnp.bfloat16

ROWS = 4
COLS = 64
TARGETS = 2560
SOURCES = 2048
BLOCK = 480
WIDTH = 7680
PLANE = 16
WIDE = 256
FAR = (2, 1, 3, 0)
FAR_FIRST = [(z, x, r) for z in FAR for x in FAR for r in (1, 2, 3, 0)]
PEERS_FIRST = [(z, x, y) for z in FAR for x in FAR for y in FAR if z or x or y]
DEEP = 256


def pieces_of(value, count):
    found = []
    rest = value
    for _ in range(count):
        piece = rest.astype(bf16).astype(f32)
        found.append(piece)
        rest = rest - piece
    return found


def spread_nodes(nodes_ref, all_ref, send_sem, recv_sem, own_sem):
    row = lax.axis_index("row")
    barrier = pltpu.get_barrier_semaphore()
    for step in range(1, ROWS):
        other = lax.rem(row + step, ROWS)
        pl.semaphore_signal(
            barrier, inc=1, device_id={"row": other}, device_id_type=MESH
        )
    own = pltpu.make_async_copy(nodes_ref, all_ref.at[row], own_sem)
    own.start()
    pl.semaphore_wait(barrier, ROWS - 1)
    copies = []
    for step in range(1, ROWS):
        other = lax.rem(row + step, ROWS)
        copy = pltpu.make_async_remote_copy(
            src_ref=nodes_ref,
            dst_ref=all_ref.at[row],
            send_sem=send_sem.at[step],
            recv_sem=recv_sem.at[step],
            device_id={"row": other},
            device_id_type=MESH,
        )
        copy.start()
        copies.append(copy)
    own.wait()
    for copy in copies:
        copy.wait()


def velocity_part(
    nodes_ref,
    order_ref,
    fibers_ref,
    forces_ref,
    out_ref,
    index_ref,
    target_ref,
    feature_ref,
    column_ref,
    source_ref,
    weight_ref,
    sum_ref,
):
    row = lax.axis_index("row")
    fibers = fibers_ref[...]
    forces = forces_ref[...]
    place = [fibers[k : k + 1] for k in range(3)]
    force = [forces[k : k + 1] for k in range(3)]
    source_square = place[0] * place[0] + place[1] * place[1] + place[2] * place[2]
    source_dot = place[0] * force[0] + place[1] * force[1] + place[2] * force[2]
    nought = jnp.zeros((1, SOURCES), f32)
    unit = jnp.ones((1, SOURCES), f32)
    near = []
    for k in range(3):
        one, two, three = pieces_of(-2.0 * place[k], 3)
        near += [one, one, two, one, three, two]
    near += [unit] * 3 + pieces_of(source_square, 3) + [nought] * 8
    source_ref[...] = jnp.concatenate(near, axis=0).T.astype(bf16)
    moments = list(force)
    for k in range(3):
        moments += [place[k] * force[m] for m in range(3)]
    moments += [source_dot] + [place[k] * source_dot for k in range(3)]
    moments += [force[k] * source_square for k in range(3)]
    moments = jnp.concatenate(moments + [nought] * 5, axis=0)
    one, two = pieces_of(moments, 2)
    weight_ref[...] = jnp.concatenate([one, two], axis=0).astype(bf16)

    index_ref[pl.ds(0, 20), :] = order_ref[row]
    index_ref[pl.ds(20, 4), :] = jnp.zeros((4, 128), jnp.int32)
    index = index_ref[...]
    high = index // 128
    low = index - high * 128
    found = tuple(jnp.zeros((24, 128), f32) for _ in range(3))

    def pick(part, found):
        found = list(found)
        for tile in range(20):
            hit = high == part * 20 + tile
            for k in range(3):
                line = nodes_ref[part, pl.ds(k, 1), pl.ds(tile * 128, 128)]
                line = jnp.broadcast_to(line, (24, 128))
                taken = jnp.take_along_axis(line, low, axis=1)
                found[k] = jnp.where(hit, taken, found[k])
        return tuple(found)

    found = lax.fori_loop(0, ROWS, pick, found)
    square = found[0] * found[0] + found[1] * found[1] + found[2] * found[2]
    lines = []
    for k in range(3):
        one, two, three = pieces_of(found[k], 3)
        lines += [one, two, one, three, one, two]
    lines += pieces_of(square, 3)
    feature_ref[...] = jnp.ones((32, TARGETS), f32)
    for slot, line in enumerate(lines):
        for tile in range(20):
            feature_ref[pl.ds(slot, 1), pl.ds(tile * 128, 128)] = line[tile : tile + 1]
    for slot, line in enumerate(list(found) + [square]):
        for tile in range(20):
            target_ref[pl.ds(slot, 1), pl.ds(tile * 128, 128)] = line[tile : tile + 1]
    column_ref[...] = feature_ref[...].astype(bf16)

    def across(turn, carry):
        at = pl.ds(pl.multiple_of(turn * WIDE, WIDE), WIDE)
        columns = column_ref[:, at]
        running = jnp.zeros((48, WIDE), f32)
        for chunk in range(SOURCES // DEEP):
            of = pl.ds(chunk * DEEP, DEEP)
            square = jnp.dot(source_ref[of, :], columns, preferred_element_type=f32)
            inverse = lax.rsqrt(square)
            cubed = inverse * inverse * inverse
            cubed_high = cubed.astype(bf16)
            cubed_low = (cubed - cubed_high.astype(f32)).astype(bf16)
            weight = weight_ref[:, of]
            running = (
                running
                + jnp.dot(weight, cubed_high, preferred_element_type=f32)
                + jnp.dot(weight, cubed_low, preferred_element_type=f32)
            )
        sum_ref[:, at] = running[:24] + running[24:]
        return carry

    lax.fori_loop(0, TARGETS // WIDE, across, 0)
    sums = sum_ref[...]
    spots = target_ref[...]
    spot = [spots[k : k + 1] for k in range(3)]
    squared = spots[3:4]
    plain = [sums[k : k + 1] for k in range(3)]
    mixed = [[sums[3 + 3 * k + m : 4 + 3 * k + m] for m in range(3)] for k in range(3)]
    along = (
        spot[0] * plain[0] + spot[1] * plain[1] + spot[2] * plain[2] - sums[12:13]
    )
    for k in range(3):
        value = squared * plain[k] + sums[16 + k : 17 + k] + spot[k] * along
        value = value + sums[13 + k : 14 + k]
        for m in range(3):
            value = value - spot[m] * (2.0 * mixed[m][k] + mixed[k][m])
        value = value * inv_eight_pi
        for tile in range(20):
            out_ref[tile * 3 + k] = value[:, tile * 128 : tile * 128 + 128]


def total_of(value):
    return jnp.sum(value, axis=1, keepdims=True)


def krylov_kernel(
    nodes_ref,
    order_ref,
    fibers_ref,
    forces_ref,
    matrix_ref,
    velocity_ref,
    density_ref,
    index_ref,
    target_ref,
    feature_ref,
    column_ref,
    source_ref,
    weight_ref,
    sum_ref,
    part_ref,
    held,
    image_one,
    image_two,
    recv_one,
    recv_two,
    recv_three,
    dots,
    recv_dots,
    piece,
    recv_piece,
    spread,
    load_sem,
    send_sems,
    recv_sems,
    dot_send,
    dot_recv,
    piece_send,
    piece_recv,
):
    row = lax.axis_index("row")
    col = lax.axis_index("col")
    level = col // PLANE
    inside = lax.rem(col, PLANE)
    load = pltpu.make_async_copy(matrix_ref, held, load_sem)
    load.start()
    piece_row = level
    piece_col = inside * 4 + row
    piece_own = jnp.logical_and(piece_row == row, piece_col == col)
    from_row = lax.rem(col, 4)
    from_col = row * PLANE + col // 4
    self_in = level == row

    barrier = pltpu.get_barrier_semaphore()

    def greet(step, carry):
        other = lax.rem(col + step, COLS)

        @pl.when(jnp.logical_not(jnp.logical_and(level == row, step == 0)))
        def _():
            pl.semaphore_signal(
                barrier, inc=1, device_id=(level, other), device_id_type=MESH
            )

        @pl.when(step > 0)
        def _():
            pl.semaphore_signal(
                barrier, inc=1, device_id=(row, other), device_id_type=MESH
            )

        return carry

    lax.fori_loop(0, COLS, greet, 0)

    @pl.when(jnp.logical_not(piece_own))
    def _():
        pl.semaphore_signal(
            barrier, inc=1, device_id=(from_row, from_col), device_id_type=MESH
        )

    lane_node = lax.broadcasted_iota(jnp.int32, (256, 512), 0)
    lane_entry = lax.broadcasted_iota(jnp.int32, (256, 512), 1)
    base = lane_entry - 3 * (lane_node - 32 * lax.rem(col, 4))
    for k in range(3):
        spread[k] = jnp.where(
            jnp.logical_and(base == k, lane_entry < BLOCK), 1.0, 0.0
        ).astype(bf16)

    velocity_part(
        nodes_ref,
        order_ref,
        fibers_ref,
        forces_ref,
        part_ref,
        index_ref,
        target_ref,
        feature_ref,
        column_ref,
        source_ref,
        weight_ref,
        sum_ref,
    )
    peers = 2 * COLS - self_in.astype(jnp.int32) - piece_own.astype(jnp.int32)
    pl.semaphore_wait(barrier, peers)

    def send_blocks(stage, source, target, stride, scale, count):
        for z_step, x_step, row_step in FAR_FIRST:
            to_x = lax.rem(col // 4 + x_step, 4)
            block = to_x * 4 + lax.rem(col + z_step, 4)
            to_row = lax.rem(row + row_step, ROWS)
            to_col = row * PLANE + block
            window = source.at[pl.ds((stride * block) // 4 * scale, count)]
            remote = pltpu.make_async_remote_copy(
                src_ref=window,
                dst_ref=target.at[col],
                send_sem=send_sems.at[stage],
                recv_sem=recv_sems.at[stage],
                device_id=(to_row, to_col),
                device_id_type=MESH,
            )
            if z_step or x_step or row_step:
                remote.start()
            else:

                @pl.when(self_in)
                def _():
                    pltpu.make_async_copy(
                        window, target.at[col], recv_sems.at[stage]
                    ).start()

                @pl.when(jnp.logical_not(self_in))
                def _():
                    remote.start()

    def await_blocks(stage, target):
        pltpu.make_async_copy(target, target, recv_sems.at[stage]).wait()

    def await_sent(stage, target):
        @pl.when(self_in)
        def _():
            some = target.at[pl.ds(0, COLS - 1)]
            pltpu.make_async_copy(some, some, send_sems.at[stage]).wait()

        @pl.when(jnp.logical_not(self_in))
        def _():
            pltpu.make_async_copy(target, target, send_sems.at[stage]).wait()

    def added(target):
        def one(step, running):
            return running + target[step]

        return lax.fori_loop(1, COLS, one, target[0], unroll=9)

    def send_piece(which, vector):
        chosen = vector[:, 0:128]
        for quarter in range(1, 4):
            chosen = jnp.where(
                row == quarter, vector[:, 120 * quarter : 120 * quarter + 128], chosen
            )
        piece[which] = chosen

        @pl.when(piece_own)
        def _():
            pltpu.make_async_copy(
                piece.at[which], recv_piece.at[which], piece_recv.at[which]
            ).start()

        @pl.when(jnp.logical_not(piece_own))
        def _():
            pltpu.make_async_remote_copy(
                src_ref=piece.at[which],
                dst_ref=recv_piece.at[which],
                send_sem=piece_send.at[which],
                recv_sem=piece_recv.at[which],
                device_id=(piece_row, piece_col),
                device_id_type=MESH,
            ).start()

    def await_piece(which):
        pltpu.make_async_copy(
            recv_piece.at[which], recv_piece.at[which], piece_recv.at[which]
        ).wait()

        @pl.when(jnp.logical_not(piece_own))
        def _():
            pltpu.make_async_copy(
                recv_piece.at[which], recv_piece.at[which], piece_send.at[which]
            ).wait()

    lane = lax.broadcasted_iota(jnp.int32, (1, 128), 1)

    def send_dots(which, values):
        line = jnp.zeros((1, 128), f32)
        for slot, value in enumerate(values):
            line = jnp.where(lane == slot, value, line)
        dots[which] = line

        for slot, (z_step, x_step, y_step) in enumerate(PEERS_FIRST):
            to_z = lax.rem(col + z_step, 4)
            to_x = lax.rem(col // 4 + x_step, 4)
            to_y = lax.rem(level + y_step, 4)
            pltpu.make_async_remote_copy(
                src_ref=dots.at[which],
                dst_ref=recv_dots.at[which, slot],
                send_sem=dot_send.at[which],
                recv_sem=dot_recv.at[which],
                device_id=(row, to_y * PLANE + to_x * 4 + to_z),
                device_id_type=MESH,
            ).start()

    def await_dots(which, count):
        whole = recv_dots.at[which]
        pltpu.make_async_copy(whole, whole, dot_recv.at[which]).wait()

        def one(step, running):
            return running + recv_dots[which, step]

        line = lax.fori_loop(0, COLS - 1, one, dots[which], unroll=9)
        return [total_of(jnp.where(lane == slot, line, 0.0)) for slot in range(count)]

    def await_dots_sent(which):
        whole = recv_dots.at[which]
        pltpu.make_async_copy(whole, whole, dot_send.at[which]).wait()

    which_row = lax.broadcasted_iota(jnp.int32, (16, 512), 0)

    def multiply(vector, image):
        high, low = pieces_of(vector, 2)
        left = jnp.where(which_row == 0, high, jnp.where(which_row == 1, low, 0.0))
        left = left.astype(bf16)[:, :BLOCK]

        for step in range(WIDTH // 512):
            got = jnp.dot(
                left, held[:, step * 512 : step * 512 + 512], preferred_element_type=f32
            )
            got = got[0:1] + got[1:2]
            for tile in range(4):
                image[step * 4 + tile] = got[:, tile * 128 : tile * 128 + 128]

    offset = lax.rem(96 * lax.rem(col, 4), 128)
    lane_wide = lax.broadcasted_iota(jnp.int32, (1, 512), 1)

    def aligned(total):
        line = jnp.concatenate([total[tile] for tile in range(5)], axis=1)
        chosen = line[:, 0:512]
        for shift in (32, 64, 96):
            chosen = jnp.where(offset == shift, line[:, shift : shift + 512], chosen)
        return jnp.where(lane_wide < BLOCK, chosen, 0.0)

    send_blocks(0, part_ref, recv_one, 5, 3, 6)
    image_one[WIDTH // 128] = jnp.zeros((1, 128), f32)
    image_two[WIDTH // 128] = jnp.zeros((1, 128), f32)
    await_blocks(0, recv_one)
    total = added(recv_one)
    which_small = lax.broadcasted_iota(jnp.int32, (16, 256), 0)
    first = jnp.zeros((16, 512), f32)
    for k in range(3):
        line = jnp.concatenate([total[k], total[3 + k]], axis=1)
        one, two, three = pieces_of(line, 3)
        left = jnp.where(
            which_small == 0,
            one,
            jnp.where(which_small == 1, two, jnp.where(which_small == 2, three, 0.0)),
        )
        first = first + jnp.dot(
            left.astype(bf16), spread[k], preferred_element_type=f32
        )
    vector = first[0:1] + first[1:2] + first[2:3]
    load.wait()
    multiply(vector, image_one)
    send_blocks(1, image_one, recv_two, 15, 1, 5)
    send_piece(0, vector)
    await_blocks(1, recv_two)
    image = aligned(added(recv_two))
    multiply(image, image_two)
    send_blocks(2, image_two, recv_three, 15, 1, 5)
    send_piece(1, image)
    send_dots(
        0, [total_of(vector * vector), total_of(vector * image), total_of(image * image)]
    )
    vv, vw, ww = await_dots(0, 3)
    norm_square = vv + tiny_eps
    initial_norm = jnp.sqrt(norm_square)
    scale_one = 1.0 / initial_norm
    entry_11 = (vv + vw) / norm_square
    slide = (vw - tiny_eps) / norm_square
    rest_square = (ww - 2.0 * slide * vw + slide * slide * vv) / norm_square
    entry_21 = jnp.sqrt(jnp.maximum(rest_square, 0.0) + tiny_eps)
    scale_two = scale_one / entry_21
    basis_one = vector * scale_one
    basis_two = (image - slide * vector) * scale_two
    await_blocks(2, recv_three)
    last = (aligned(added(recv_three)) - slide * image) * scale_two
    send_dots(
        1,
        [
            total_of(basis_one * basis_one),
            total_of(basis_one * basis_two),
            total_of(basis_two * basis_two),
            total_of(basis_one * last),
            total_of(basis_two * last),
            total_of(last * last),
        ],
    )
    await_piece(0)
    await_piece(1)
    velocity_piece = recv_piece[0]
    image_piece = recv_piece[1]
    velocity_ref[...] = velocity_piece[:, :120]
    aa, ab, bb, al, bl, ll = await_dots(1, 6)
    entry_12 = ab + al
    entry_22 = bb + bl - entry_12 * ab
    from_one = -entry_12
    from_two = 1.0 - entry_22
    rest_two = (
        ll
        + from_one * from_one * aa
        + from_two * from_two * bb
        + 2.0 * (from_one * from_two * ab + from_one * al + from_two * bl)
    )
    entry_32 = jnp.sqrt(jnp.maximum(rest_two, 0.0) + tiny_eps)
    radius_one = jnp.sqrt(entry_11 * entry_11 + entry_21 * entry_21)
    cosine_one = entry_11 / radius_one
    sine_one = entry_21 / radius_one
    upper_12 = cosine_one * entry_12 + sine_one * entry_22
    lower_22 = cosine_one * entry_22 - sine_one * entry_12
    radius_two = jnp.sqrt(lower_22 * lower_22 + entry_32 * entry_32)
    weight_two = lower_22 / radius_two * (-sine_one * initial_norm) / radius_two
    weight_one = (cosine_one * initial_norm - upper_12 * weight_two) / radius_one
    result = weight_one * (velocity_piece * scale_one) + weight_two * (
        (image_piece - slide * velocity_piece) * scale_two
    )
    density_ref[...] = result[:, :120]
    await_sent(0, recv_one)
    await_sent(1, recv_two)
    await_sent(2, recv_three)
    await_dots_sent(0)
    await_dots_sent(1)


def in_vmem(count):
    return [pl.BlockSpec(memory_space=pltpu.VMEM)] * count


def shards(matrix_t, fibers, forces, nodes, node_order):
    all_nodes = pl.pallas_call(
        spread_nodes,
        name="spread_nodes",
        out_shape=jax.ShapeDtypeStruct((ROWS, 3, TARGETS), f32),
        in_specs=in_vmem(1),
        out_specs=in_vmem(1)[0],
        scratch_shapes=[
            pltpu.SemaphoreType.DMA((ROWS,)),
            pltpu.SemaphoreType.DMA((ROWS,)),
            pltpu.SemaphoreType.DMA,
        ],
        compiler_params=pltpu.CompilerParams(collective_id=0, has_side_effects=True),
    )(nodes)
    velocity, density = pl.pallas_call(
        krylov_kernel,
        name="krylov",
        out_shape=[jax.ShapeDtypeStruct((1, 120), f32)] * 2,
        in_specs=in_vmem(4) + [pl.BlockSpec(memory_space=pl.ANY)],
        out_specs=in_vmem(2),
        scratch_shapes=[
            pltpu.VMEM((24, 128), jnp.int32),
            pltpu.VMEM((8, TARGETS), f32),
            pltpu.VMEM((32, TARGETS), f32),
            pltpu.VMEM((32, TARGETS), bf16),
            pltpu.VMEM((SOURCES, 32), bf16),
            pltpu.VMEM((48, SOURCES), bf16),
            pltpu.VMEM((24, TARGETS), f32),
            pltpu.VMEM((WIDTH // 128, 1, 128), f32),
            pltpu.VMEM((BLOCK, WIDTH), bf16),
            pltpu.VMEM((WIDTH // 128 + 1, 1, 128), f32),
            pltpu.VMEM((WIDTH // 128 + 1, 1, 128), f32),
            pltpu.VMEM((COLS, 6, 1, 128), f32),
            pltpu.VMEM((COLS, 5, 1, 128), f32),
            pltpu.VMEM((COLS, 5, 1, 128), f32),
            pltpu.VMEM((2, 1, 128), f32),
            pltpu.VMEM((2, COLS - 1, 1, 128), f32),
            pltpu.VMEM((2, 1, 128), f32),
            pltpu.VMEM((2, 1, 128), f32),
            pltpu.VMEM((3, 256, 512), bf16),
            pltpu.SemaphoreType.DMA,
            pltpu.SemaphoreType.DMA((3,)),
            pltpu.SemaphoreType.DMA((3,)),
            pltpu.SemaphoreType.DMA((2,)),
            pltpu.SemaphoreType.DMA((2,)),
            pltpu.SemaphoreType.DMA((2,)),
            pltpu.SemaphoreType.DMA((2,)),
        ],
        compiler_params=pltpu.CompilerParams(collective_id=1, has_side_effects=True),
    )(all_nodes, node_order.reshape(ROWS, 20, 128), fibers, forces, matrix_t)
    return velocity.reshape(120), density.reshape(120)


def solution(mesh):
    return jax.shard_map(
        shards,
        mesh=mesh,
        in_specs=(P("col", "row"), P(None, "col"), P(None, "col"), P(None, "row"), P()),
        out_specs=(P(("row", "col")), P(("row", "col"))),
        check_vma=False,
    )
```

```python
import math

import jax
import jax.numpy as jnp
from jax import lax
from jax.experimental import pallas as pl
from jax.experimental.pallas import tpu as pltpu
from jax.sharding import PartitionSpec as P

MESH = pl.DeviceIdType.MESH
inv_eight_pi = 1.0 / (8.0 * math.pi)
tiny_eps = 1e-06
f32 = jnp.float32
bf16 = jnp.bfloat16

ROWS = 4
COLS = 64
TARGETS = 2560
SOURCES = 2048
BLOCK = 480
WIDTH = 7680
PLANE = 16
WIDE = 256
FAR = (2, 1, 3, 0)
FAR_FIRST = [(z, x, r) for z in FAR for x in FAR for r in (1, 2, 3, 0)]
PEERS_FIRST = [(z, x, y) for z in FAR for x in FAR for y in FAR if z or x or y]
DEEP = 256


def pieces_of(value, count):
    found = []
    rest = value
    for _ in range(count):
        piece = rest.astype(bf16).astype(f32)
        found.append(piece)
        rest = rest - piece
    return found


def prepare_sources(fibers_ref, forces_ref, source_ref, weight_ref):
    fibers = fibers_ref[...]
    forces = forces_ref[...]
    place = [fibers[k : k + 1] for k in range(3)]
    force = [forces[k : k + 1] for k in range(3)]
    source_square = place[0] * place[0] + place[1] * place[1] + place[2] * place[2]
    source_dot = place[0] * force[0] + place[1] * force[1] + place[2] * force[2]
    nought = jnp.zeros((1, SOURCES), f32)
    unit = jnp.ones((1, SOURCES), f32)
    near = []
    for k in range(3):
        one, two, three = pieces_of(-2.0 * place[k], 3)
        near += [one, one, two, one, three, two]
    near += [unit] * 3 + pieces_of(source_square, 3) + [nought] * 8
    source_ref[...] = jnp.concatenate(near, axis=0).T.astype(bf16)
    moments = list(force)
    for k in range(3):
        moments += [place[k] * force[m] for m in range(3)]
    moments += [source_dot] + [place[k] * source_dot for k in range(3)]
    moments += [force[k] * source_square for k in range(3)]
    moments = jnp.concatenate(moments + [nought] * 5, axis=0)
    one, two = pieces_of(moments, 2)
    weight_ref[...] = jnp.concatenate([one, two], axis=0).astype(bf16)


def indices(row, order_ref, index_ref):
    index_ref[pl.ds(0, 20), :] = order_ref[pl.ds(row * 20, 20), :]
    index_ref[pl.ds(20, 4), :] = jnp.zeros((4, 128), jnp.int32)
    index = index_ref[...]
    high = index // 128
    return high, index - high * 128


def pick(part, nodes, high, low, found):
    found = list(found)
    for tile in range(20):
        hit = high == part * 20 + tile
        for k in range(3):
            line = nodes[pl.ds(k, 1), pl.ds(tile * 128, 128)]
            line = jnp.broadcast_to(line, (24, 128))
            taken = jnp.take_along_axis(line, low, axis=1)
            found[k] = jnp.where(hit, taken, found[k])
    return found


def velocity_part(
    found,
    between,
    out_ref,
    target_ref,
    feature_ref,
    column_ref,
    source_ref,
    weight_ref,
    sum_ref,
):
    square = found[0] * found[0] + found[1] * found[1] + found[2] * found[2]
    lines = []
    for k in range(3):
        one, two, three = pieces_of(found[k], 3)
        lines += [one, two, one, three, one, two]
    lines += pieces_of(square, 3)
    feature_ref[...] = jnp.ones((32, TARGETS), f32)
    for slot, line in enumerate(lines):
        for tile in range(20):
            feature_ref[pl.ds(slot, 1), pl.ds(tile * 128, 128)] = line[tile : tile + 1]
    for slot, line in enumerate(list(found) + [square]):
        for tile in range(20):
            target_ref[pl.ds(slot, 1), pl.ds(tile * 128, 128)] = line[tile : tile + 1]
    column_ref[...] = feature_ref[...].astype(bf16)

    def across(turn, carry):
        between(turn)
        at = pl.ds(pl.multiple_of(turn * WIDE, WIDE), WIDE)
        columns = column_ref[:, at]
        running = jnp.zeros((48, WIDE), f32)
        for chunk in range(SOURCES // DEEP):
            of = pl.ds(chunk * DEEP, DEEP)
            square = jnp.dot(source_ref[of, :], columns, preferred_element_type=f32)
            inverse = lax.rsqrt(square)
            cubed = inverse * inverse * inverse
            cubed_high = cubed.astype(bf16)
            cubed_low = (cubed - cubed_high.astype(f32)).astype(bf16)
            weight = weight_ref[:, of]
            running = (
                running
                + jnp.dot(weight, cubed_high, preferred_element_type=f32)
                + jnp.dot(weight, cubed_low, preferred_element_type=f32)
            )
        sum_ref[:, at] = running[:24] + running[24:]
        return carry

    lax.fori_loop(0, TARGETS // WIDE, across, 0)
    sums = sum_ref[...]
    spots = target_ref[...]
    spot = [spots[k : k + 1] for k in range(3)]
    squared = spots[3:4]
    plain = [sums[k : k + 1] for k in range(3)]
    mixed = [[sums[3 + 3 * k + m : 4 + 3 * k + m] for m in range(3)] for k in range(3)]
    along = (
        spot[0] * plain[0] + spot[1] * plain[1] + spot[2] * plain[2] - sums[12:13]
    )
    for k in range(3):
        value = squared * plain[k] + sums[16 + k : 17 + k] + spot[k] * along
        value = value + sums[13 + k : 14 + k]
        for m in range(3):
            value = value - spot[m] * (2.0 * mixed[m][k] + mixed[k][m])
        value = value * inv_eight_pi
        for tile in range(20):
            out_ref[tile * 3 + k] = value[:, tile * 128 : tile * 128 + 128]


def total_of(value):
    return jnp.sum(value, axis=1, keepdims=True)


def krylov_kernel(
    nodes_ref,
    order_ref,
    fibers_ref,
    forces_ref,
    matrix_ref,
    result_ref,
    index_ref,
    target_ref,
    feature_ref,
    column_ref,
    source_ref,
    weight_ref,
    sum_ref,
    all_ref,
    part_ref,
    held,
    image_one,
    image_two,
    recv_one,
    recv_two,
    recv_three,
    dots,
    recv_dots,
    piece,
    recv_piece,
    spread,
    load_sem,
    send_sems,
    recv_sems,
    dot_send,
    dot_recv,
    piece_send,
    piece_recv,
    node_send,
    node_recv,
    round_sem,
):
    row = lax.axis_index("row")
    col = lax.axis_index("col")
    level = col // PLANE
    inside = lax.rem(col, PLANE)
    load = pltpu.make_async_copy(matrix_ref, held, load_sem)
    load.start()
    piece_row = level
    piece_col = inside * 4 + row
    piece_own = jnp.logical_and(piece_row == row, piece_col == col)
    from_row = lax.rem(col, 4)
    from_col = row * PLANE + col // 4
    self_in = level == row

    mate = row + 1 - 2 * lax.rem(row, 2)
    row_peers = [mate, lax.rem(row + 2, ROWS), lax.rem(mate + 2, ROWS)]
    x_at = lax.rem(col // 4, 4)
    z_at = lax.rem(col, 4)

    def device(x, y, z):
        return (row, y * PLANE + x * 4 + z)

    x_line = [device(lax.rem(x_at + k, 4), level, z_at) for k in (1, 2, 3)]
    y_line = [device(x_at, lax.rem(level + k, 4), z_at) for k in (1, 2, 3)]
    z_near = [device(x_at, level, lax.rem(z_at + k, 4)) for k in (1, 3)]

    barrier = pltpu.get_barrier_semaphore()
    near = [(peer, col) for peer in row_peers] + x_line + y_line + z_near
    for peer in near:
        pl.semaphore_signal(barrier, inc=1, device_id=peer, device_id_type=MESH)

    def tell(which, peers):
        for peer in peers:
            pl.semaphore_signal(
                round_sem.at[which], inc=1, device_id=peer, device_id_type=MESH
            )

    lane_node = lax.broadcasted_iota(jnp.int32, (256, 512), 0)
    lane_entry = lax.broadcasted_iota(jnp.int32, (256, 512), 1)
    base = lane_entry - 3 * (lane_node - 32 * lax.rem(col, 4))
    for k in range(3):
        spread[k] = jnp.where(
            jnp.logical_and(base == k, lane_entry < BLOCK), 1.0, 0.0
        ).astype(bf16)

    prepare_sources(fibers_ref, forces_ref, source_ref, weight_ref)
    high, low = indices(row, order_ref, index_ref)
    pl.semaphore_wait(barrier, len(near))
    node_copies = [
        pltpu.make_async_remote_copy(
            src_ref=nodes_ref,
            dst_ref=all_ref.at[slot],
            send_sem=node_send.at[slot],
            recv_sem=node_recv.at[slot],
            device_id=(peer, col),
            device_id_type=MESH,
        )
        for slot, peer in enumerate(row_peers)
    ]
    for copy in node_copies:
        copy.start()
    tell(0, x_line)
    found = pick(row, nodes_ref, high, low, [jnp.zeros((24, 128), f32)] * 3)
    for slot, peer in enumerate(row_peers):
        node_copies[slot].wait_recv()
        found = pick(peer, all_ref.at[slot], high, low, found)

    rounds = [x_line, y_line, z_near, z_near]

    def between(turn):
        for which in range(3):

            @pl.when(turn == 2 * which + 1)
            def _():
                pl.semaphore_wait(round_sem.at[which], len(rounds[which]))
                tell(which + 1, rounds[which + 1])

    velocity_part(
        found,
        between,
        part_ref,
        target_ref,
        feature_ref,
        column_ref,
        source_ref,
        weight_ref,
        sum_ref,
    )
    pl.semaphore_wait(round_sem.at[3], len(z_near))

    def send_blocks(stage, source, target, stride, scale, count):
        for z_step, x_step, row_step in FAR_FIRST:
            to_x = lax.rem(col // 4 + x_step, 4)
            block = to_x * 4 + lax.rem(col + z_step, 4)
            to_row = lax.rem(row + row_step, ROWS)
            to_col = row * PLANE + block
            window = source.at[pl.ds((stride * block) // 4 * scale, count)]
            remote = pltpu.make_async_remote_copy(
                src_ref=window,
                dst_ref=target.at[col],
                send_sem=send_sems.at[stage],
                recv_sem=recv_sems.at[stage],
                device_id=(to_row, to_col),
                device_id_type=MESH,
            )
            if z_step or x_step or row_step:
                remote.start()
            else:

                @pl.when(self_in)
                def _():
                    pltpu.make_async_copy(
                        window, target.at[col], recv_sems.at[stage]
                    ).start()

                @pl.when(jnp.logical_not(self_in))
                def _():
                    remote.start()

    def await_blocks(stage, target):
        pltpu.make_async_copy(target, target, recv_sems.at[stage]).wait()

    def await_sent(stage, target):
        @pl.when(self_in)
        def _():
            some = target.at[pl.ds(0, COLS - 1)]
            pltpu.make_async_copy(some, some, send_sems.at[stage]).wait()

        @pl.when(jnp.logical_not(self_in))
        def _():
            pltpu.make_async_copy(target, target, send_sems.at[stage]).wait()

    def added(target):
        def one(step, running):
            return running + target[step]

        return lax.fori_loop(1, COLS, one, target[0], unroll=9)

    def send_piece(which, vector):
        chosen = vector[:, 0:128]
        for quarter in range(1, 4):
            chosen = jnp.where(
                row == quarter, vector[:, 120 * quarter : 120 * quarter + 128], chosen
            )
        piece[which] = chosen

        @pl.when(piece_own)
        def _():
            pltpu.make_async_copy(
                piece.at[which], recv_piece.at[which], piece_recv.at[which]
            ).start()

        @pl.when(jnp.logical_not(piece_own))
        def _():
            pltpu.make_async_remote_copy(
                src_ref=piece.at[which],
                dst_ref=recv_piece.at[which],
                send_sem=piece_send.at[which],
                recv_sem=piece_recv.at[which],
                device_id=(piece_row, piece_col),
                device_id_type=MESH,
            ).start()

    def await_piece(which):
        pltpu.make_async_copy(
            recv_piece.at[which], recv_piece.at[which], piece_recv.at[which]
        ).wait()

        @pl.when(jnp.logical_not(piece_own))
        def _():
            pltpu.make_async_copy(
                recv_piece.at[which], recv_piece.at[which], piece_send.at[which]
            ).wait()

    lane = lax.broadcasted_iota(jnp.int32, (1, 128), 1)

    def send_dots(which, values):
        line = jnp.zeros((1, 128), f32)
        for slot, value in enumerate(values):
            line = jnp.where(lane == slot, value, line)
        dots[which] = line

        for slot, (z_step, x_step, y_step) in enumerate(PEERS_FIRST):
            to_z = lax.rem(col + z_step, 4)
            to_x = lax.rem(col // 4 + x_step, 4)
            to_y = lax.rem(level + y_step, 4)
            pltpu.make_async_remote_copy(
                src_ref=dots.at[which],
                dst_ref=recv_dots.at[which, slot],
                send_sem=dot_send.at[which],
                recv_sem=dot_recv.at[which],
                device_id=(row, to_y * PLANE + to_x * 4 + to_z),
                device_id_type=MESH,
            ).start()

    def await_dots(which, count):
        whole = recv_dots.at[which]
        pltpu.make_async_copy(whole, whole, dot_recv.at[which]).wait()

        def one(step, running):
            return running + recv_dots[which, step]

        line = lax.fori_loop(0, COLS - 1, one, dots[which], unroll=9)
        return [total_of(jnp.where(lane == slot, line, 0.0)) for slot in range(count)]

    def await_dots_sent(which):
        whole = recv_dots.at[which]
        pltpu.make_async_copy(whole, whole, dot_send.at[which]).wait()

    which_row = lax.broadcasted_iota(jnp.int32, (16, 512), 0)

    def multiply(vector, image):
        high, low = pieces_of(vector, 2)
        left = jnp.where(which_row == 0, high, jnp.where(which_row == 1, low, 0.0))
        left = left.astype(bf16)[:, :BLOCK]

        for step in range(WIDTH // 512):
            got = jnp.dot(
                left, held[:, step * 512 : step * 512 + 512], preferred_element_type=f32
            )
            got = got[0:1] + got[1:2]
            for tile in range(4):
                image[step * 4 + tile] = got[:, tile * 128 : tile * 128 + 128]

    offset = lax.rem(96 * lax.rem(col, 4), 128)
    lane_wide = lax.broadcasted_iota(jnp.int32, (1, 512), 1)

    def aligned(total):
        line = jnp.concatenate([total[tile] for tile in range(5)], axis=1)
        chosen = line[:, 0:512]
        for shift in (32, 64, 96):
            chosen = jnp.where(offset == shift, line[:, shift : shift + 512], chosen)
        return jnp.where(lane_wide < BLOCK, chosen, 0.0)

    send_blocks(0, part_ref, recv_one, 5, 3, 6)
    image_one[WIDTH // 128] = jnp.zeros((1, 128), f32)
    image_two[WIDTH // 128] = jnp.zeros((1, 128), f32)
    await_blocks(0, recv_one)
    total = added(recv_one)
    which_small = lax.broadcasted_iota(jnp.int32, (16, 256), 0)
    first = jnp.zeros((16, 512), f32)
    for k in range(3):
        line = jnp.concatenate([total[k], total[3 + k]], axis=1)
        one, two, three = pieces_of(line, 3)
        left = jnp.where(
            which_small == 0,
            one,
            jnp.where(which_small == 1, two, jnp.where(which_small == 2, three, 0.0)),
        )
        first = first + jnp.dot(
            left.astype(bf16), spread[k], preferred_element_type=f32
        )
    vector = first[0:1] + first[1:2] + first[2:3]
    load.wait()
    multiply(vector, image_one)
    send_blocks(1, image_one, recv_two, 15, 1, 5)
    send_piece(0, vector)
    await_blocks(1, recv_two)
    image = aligned(added(recv_two))
    multiply(image, image_two)
    send_blocks(2, image_two, recv_three, 15, 1, 5)
    send_piece(1, image)
    send_dots(
        0, [total_of(vector * vector), total_of(vector * image), total_of(image * image)]
    )
    vv, vw, ww = await_dots(0, 3)
    norm_square = vv + tiny_eps
    initial_norm = jnp.sqrt(norm_square)
    scale_one = 1.0 / initial_norm
    entry_11 = (vv + vw) / norm_square
    slide = (vw - tiny_eps) / norm_square
    rest_square = (ww - 2.0 * slide * vw + slide * slide * vv) / norm_square
    entry_21 = jnp.sqrt(jnp.maximum(rest_square, 0.0) + tiny_eps)
    scale_two = scale_one / entry_21
    basis_one = vector * scale_one
    basis_two = (image - slide * vector) * scale_two
    await_blocks(2, recv_three)
    last = (aligned(added(recv_three)) - slide * image) * scale_two
    send_dots(
        1,
        [
            total_of(basis_one * basis_one),
            total_of(basis_one * basis_two),
            total_of(basis_two * basis_two),
            total_of(basis_one * last),
            total_of(basis_two * last),
            total_of(last * last),
        ],
    )
    await_piece(0)
    await_piece(1)
    velocity_piece = recv_piece[0]
    image_piece = recv_piece[1]
    aa, ab, bb, al, bl, ll = await_dots(1, 6)
    entry_12 = ab + al
    entry_22 = bb + bl - entry_12 * ab
    from_one = -entry_12
    from_two = 1.0 - entry_22
    rest_two = (
        ll
        + from_one * from_one * aa
        + from_two * from_two * bb
        + 2.0 * (from_one * from_two * ab + from_one * al + from_two * bl)
    )
    entry_32 = jnp.sqrt(jnp.maximum(rest_two, 0.0) + tiny_eps)
    radius_one = jnp.sqrt(entry_11 * entry_11 + entry_21 * entry_21)
    cosine_one = entry_11 / radius_one
    sine_one = entry_21 / radius_one
    upper_12 = cosine_one * entry_12 + sine_one * entry_22
    lower_22 = cosine_one * entry_22 - sine_one * entry_12
    radius_two = jnp.sqrt(lower_22 * lower_22 + entry_32 * entry_32)
    weight_two = lower_22 / radius_two * (-sine_one * initial_norm) / radius_two
    weight_one = (cosine_one * initial_norm - upper_12 * weight_two) / radius_one
    result = weight_one * (velocity_piece * scale_one) + weight_two * (
        (image_piece - slide * velocity_piece) * scale_two
    )
    result_ref[pl.ds(0, 1), :] = velocity_piece
    result_ref[pl.ds(1, 1), :] = result
    for copy in node_copies:
        copy.wait_send()
    await_sent(0, recv_one)
    await_sent(1, recv_two)
    await_sent(2, recv_three)
    await_dots_sent(0)
    await_dots_sent(1)


def in_vmem(count):
    return [pl.BlockSpec(memory_space=pltpu.VMEM)] * count


def shards(matrix_t, fibers, forces, nodes, node_order):
    result = pl.pallas_call(
        krylov_kernel,
        name="krylov",
        out_shape=jax.ShapeDtypeStruct((2, 128), f32),
        in_specs=in_vmem(4) + [pl.BlockSpec(memory_space=pl.ANY)],
        out_specs=in_vmem(1)[0],
        scratch_shapes=[
            pltpu.VMEM((24, 128), jnp.int32),
            pltpu.VMEM((8, TARGETS), f32),
            pltpu.VMEM((32, TARGETS), f32),
            pltpu.VMEM((32, TARGETS), bf16),
            pltpu.VMEM((SOURCES, 32), bf16),
            pltpu.VMEM((48, SOURCES), bf16),
            pltpu.VMEM((24, TARGETS), f32),
            pltpu.VMEM((3, 3, TARGETS), f32),
            pltpu.VMEM((WIDTH // 128, 1, 128), f32),
            pltpu.VMEM((BLOCK, WIDTH), bf16),
            pltpu.VMEM((WIDTH // 128 + 1, 1, 128), f32),
            pltpu.VMEM((WIDTH // 128 + 1, 1, 128), f32),
            pltpu.VMEM((COLS, 6, 1, 128), f32),
            pltpu.VMEM((COLS, 5, 1, 128), f32),
            pltpu.VMEM((COLS, 5, 1, 128), f32),
            pltpu.VMEM((2, 1, 128), f32),
            pltpu.VMEM((2, COLS - 1, 1, 128), f32),
            pltpu.VMEM((2, 1, 128), f32),
            pltpu.VMEM((2, 1, 128), f32),
            pltpu.VMEM((3, 256, 512), bf16),
            pltpu.SemaphoreType.DMA,
            pltpu.SemaphoreType.DMA((3,)),
            pltpu.SemaphoreType.DMA((3,)),
            pltpu.SemaphoreType.DMA((2,)),
            pltpu.SemaphoreType.DMA((2,)),
            pltpu.SemaphoreType.DMA((2,)),
            pltpu.SemaphoreType.DMA((2,)),
            pltpu.SemaphoreType.DMA((3,)),
            pltpu.SemaphoreType.DMA((3,)),
            pltpu.SemaphoreType.REGULAR((4,)),
        ],
        compiler_params=pltpu.CompilerParams(collective_id=0, has_side_effects=True),
    )(nodes, node_order.reshape(80, 128), fibers, forces, matrix_t)
    return result[0, :120], result[1, :120]


def solution(mesh):
    return jax.shard_map(
        shards,
        mesh=mesh,
        in_specs=(P("col", "row"), P(None, "col"), P(None, "col"), P(None, "row"), P()),
        out_specs=(P(("row", "col")), P(("row", "col"))),
        check_vma=False,
    )
```
